32 devices in a mesh: gx: 8 (over z, core), gy: 4 (over y, x).
Axes of the slice: x: 2, y: 2, z: 4, core: 2. Of those that a mesh axis runs over, the one named last changes fastest.
Arguments:
- ensemble: float32 [80, 192, 512], P(None, 'gx', 'gy'), may hold values from -6 to 6
- obs_values: float32 [3, 1024], replicated, may hold values from -8 to 8
- obs_error: float32 [3, 1024], replicated, may hold values from 0.2 to 2
- obs_cell: int32 [3, 1024], replicated, may hold values from 0 to 3071
- band_offsets: int32 [3], replicated, may hold values from 24 to 71
Outputs:
- analysis: float32 [80, 192, 512], P(None, 'gx', 'gy')
The draws below stay inside these ranges and needn't reach their ends.
Inputs may be any that keep to these rules, and one draw needn't show every extreme that they name: `obs_cell`: an observation of device p lies in p's own tile.
All inputs are finite; a program needn't handle non-finite values.
Results may differ from the reference program's by a relative error of at most 0.011.
Values sent between devices are 32-bit elements; how exact they have to be, the bound alone decides.
No kernel may reach another device: no remote copies, remote signals or barrier semaphores. Data moves between devices by JAX's collectives and lax.ppermute only.
A program may use at most 64 MiB of HBM per device.

```python
import math
import jax
import jax.numpy as jnp
from jax import lax

MEMBERS = 80
LEVELS = 8
CY = 16
CX = 24
OBS_DEV = 32
BATCHES = 3
OBS = 1024
NX = 192
NY = 64
N_GY = 4


def draw_band_offsets(key, part):
    values = jax.random.randint(key, (BATCHES,), CX, 3 * CX)
    where_top = jax.random.randint(jax.random.fold_in(key, 7), (), 0, BATCHES)
    values = values.at[where_top].set(3 * CX - 1)
    values = values.at[(where_top + 1) % BATCHES].set(CX)
    return values.astype(jnp.int32)


def set_ends(drawn, rng, low, top_value):
    dims = drawn.shape
    spot = [jax.random.randint(jax.random.fold_in(rng, axis), (), 0, dims[axis]) for axis in range(len(dims))]
    drawn = drawn.at[tuple(spot)].set(low)
    longest = dims.index(max(dims))
    spot[longest] = (spot[longest] + 1) % dims[longest]
    return drawn.at[tuple(spot)].set(top_value)


def shard_levels(stream_key, shape, split, least, top_value):
    loudness = 1.0
    for dim, parts in split:
        heights = jax.random.uniform(jax.random.fold_in(jax.random.fold_in(stream_key, 6), dim), (parts,), jnp.float32, least / len(split), top_value / len(split))
        loudness = loudness * jnp.repeat(jnp.exp(heights), shape[dim] // parts).reshape((-1,) + (1,) * (len(shape) - 1 - dim))
    return loudness


def scatter_about(key, dims, width, reach, split=(), kind=jnp.bfloat16):
    array = jax.random.normal(key, dims, jnp.float32) * width
    if len(split) > 0:
        array = shard_levels(key, dims, split, -0.22, 0.18) * array
    return jnp.clip(array, min=-reach, max=reach).astype(kind)


def setup_inputs(seed: int = 0) -> dict:
    key_of = jax.random.split(jax.random.key(seed), 6)
    ensemble = scatter_about(key_of[0], (MEMBERS, NX, NY * LEVELS), 1.0, 6.0, ((1, 8), (2, 4)), jnp.float32)
    obs_values = scatter_about(key_of[1], (BATCHES, OBS), 1.5, 8.0, (), jnp.float32)
    obs_error = jnp.clip(jnp.exp(jax.random.uniform(key_of[2], (BATCHES, OBS), jnp.float32, math.log(0.2), math.log(2.0))), 0.2, 2.0)
    obs_cell = set_ends(jax.random.randint(key_of[3], (BATCHES, OBS), 0, CX * CY * LEVELS), jax.random.fold_in(key_of[3], 1), 0, (CX * CY * LEVELS) - 1).astype(jnp.int32)
    band_offsets = draw_band_offsets(jax.random.fold_in(key_of[5], 71), 0)
    return dict(ensemble=ensemble, obs_values=obs_values, obs_error=obs_error, obs_cell=obs_cell, band_offsets=band_offsets)


def taper(distance, radius):
    ratio = distance / radius
    return jnp.where(ratio < 1.0, (1.0 - ratio) ** 2 * (1.0 + 2.0 * ratio), 0.0)

def locate(obs_index, cell_ids, gy_count):
    owner = obs_index // OBS_DEV
    column_len = CY * LEVELS
    obs_x = owner // gy_count * CX + cell_ids // column_len
    obs_y = owner % gy_count * CY + cell_ids % column_len // LEVELS
    return (obs_x, obs_y)

def statistics(panel_now, errors, values):
    members = panel_now.shape[0]
    obs_mean = lax.optimization_barrier(jnp.mean(panel_now, axis=0))
    deviate = panel_now - obs_mean
    variance = lax.optimization_barrier(jnp.sum(deviate * deviate, axis=0)) / (members - 1)
    total_var = variance + errors
    scaling = 1.0 / ((members - 1) * total_var)
    shrink = 1.0 / (1.0 + jnp.sqrt(errors / total_var))
    weighted = jnp.concatenate([shrink * deviate, (values - obs_mean)[None, :]], axis=0).astype(jnp.bfloat16)
    return (deviate.astype(jnp.bfloat16), scaling, weighted)

def update_cells(columns, cell_x, cell_y, obs_x, obs_y, radius, extent, packed):
    pert_obs, scaling, weighted = packed
    members = columns.shape[0]
    ens_mean = lax.optimization_barrier(jnp.mean(columns, axis=0))
    spread = columns - ens_mean
    covar = lax.dot_general(spread.astype(jnp.bfloat16), pert_obs, (((0,), (0,)), ((), ())), preferred_element_type=jnp.float32)
    gap_x = jnp.abs(cell_x[:, None] - obs_x[None, :])
    gap_x = jnp.minimum(gap_x, extent - gap_x)
    gap_y = jnp.abs(cell_y[:, None] - obs_y[None, :])
    weights = taper(gap_x.astype(jnp.float32), radius) * taper(gap_y.astype(jnp.float32), radius)
    gain_wts = (weights * covar * scaling[None, :]).astype(jnp.bfloat16)
    increment = lax.dot_general(weighted, gain_wts, (((1,), (1,)), ((), ())), preferred_element_type=jnp.float32)
    return ens_mean + increment[members] + spread - increment[:members]

def reference(ensemble, obs_values, obs_error, obs_cell, band_offsets):
    obs_index = jnp.arange(OBS, dtype=jnp.int32)
    cell_y = jnp.arange(NY * LEVELS, dtype=jnp.int32) // LEVELS
    analysis = ensemble
    for batch_id in range(BATCHES):
        cell_ids = obs_cell[batch_id]
        obs_x, obs_y = locate(obs_index, cell_ids, N_GY)
        flat_col = obs_y * LEVELS + cell_ids % LEVELS
        prior_now = analysis[:, obs_x, flat_col]
        packed = statistics(prior_now, obs_error[batch_id], obs_values[batch_id])
        radius = band_offsets[batch_id].astype(jnp.float32)
        current = analysis

        def one_row(row_id):
            columns = lax.dynamic_index_in_dim(current, row_id, 1, keepdims=False)
            cell_x = jnp.full(cell_y.shape, row_id, dtype=jnp.int32)
            return update_cells(columns, cell_x, cell_y, obs_x, obs_y, radius, NX, packed)
        rows_new = lax.map(one_row, jnp.arange(NX, dtype=jnp.int32))
        analysis = jnp.transpose(rows_new, (1, 0, 2))
    return analysis
```

```python
import functools

import jax
import jax.numpy as jnp
from jax import lax
from jax.experimental import pallas as pl
from jax.experimental.pallas import tpu as pltpu
from jax.sharding import PartitionSpec as P

LEVELS = 8
CY = 16
CX = 24
OBS_DEV = 32
LANES = 128
MEAN, XPOS, YPOS, ERR, VAL = 80, 81, 82, 83, 84
BLOCK_OBS = 256


def pick_kernel(gx_count, gy_count, members, batches, pos, cell, error, value, x_ref, z_ref, g_ref):
    cells_x, column = CX, CY * LEVELS
    sub = lax.broadcasted_iota(jnp.int32, (8, column), 0)
    for x in range(cells_x):
        block = x_ref[pl.ds(x, members, stride=cells_x), :]
        mean = jnp.sum(block, axis=0, keepdims=True) * (1.0 / members)
        mean_rows = jnp.where(sub == 0, mean, 0.0)
        rest = jnp.zeros((LANES - members - 8, column), jnp.float32)
        full = jnp.concatenate([block - mean, mean_rows, rest], axis=0)
        z_ref[x * column : (x + 1) * column, :] = full.T
    lane = lax.broadcasted_iota(jnp.int32, (1, LANES), 1)
    first = (pos[0] * gy_count + pos[1]) * OBS_DEV
    for b in range(batches):
        for r in range(OBS_DEV):
            c = cell[b, first + r]
            row = z_ref[pl.ds(c, 1), :]
            ox = (pos[0] * CX + c // column).astype(jnp.float32)
            oy = (pos[1] * CY + c % column // LEVELS).astype(jnp.float32)
            row = jnp.where(lane == XPOS, ox, row)
            row = jnp.where(lane == YPOS, oy, row)
            row = jnp.where(lane == ERR, error[b, first + r], row)
            row = jnp.where(lane == VAL, value[b, first + r], row)
            g_ref[b * OBS_DEV + r : b * OBS_DEV + r + 1, :] = row


def taper(distance, inverse):
    left = jnp.maximum(1.0 - distance * inverse, 0.0)
    return left * left * (3.0 - 2.0 * left)


def sweep_kernel(gx_count, gy_count, members, batches, masks, pos, radius, *refs):
    gathered, (z_in, out_ref, z, cells, rows, obs_cells, hp, rhs, line) = refs[:-9], refs[-9:]
    column = CY * LEVELS
    own_rows = batches * OBS_DEV
    group = gy_count * OBS_DEV
    per_block = max(1, BLOCK_OBS // group)
    block = per_block * group
    obs = gx_count * group
    extent = float(gx_count * CX)
    gx, gy = pos[0], pos[1]

    here = 0
    for part in gathered:
        for i in range(part.shape[0] // own_rows):
            mx, my = masks[here]
            here += 1
            owner = (gx ^ mx) * gy_count + (gy ^ my)
            for b in range(batches):
                rows[b, pl.ds(pl.multiple_of(owner * OBS_DEV, OBS_DEV), OBS_DEV), :] = part[
                    i * own_rows + b * OBS_DEV : i * own_rows + (b + 1) * OBS_DEV, :
                ]

    sub16 = lax.broadcasted_iota(jnp.int32, (16, LANES), 0)
    sub8 = lax.broadcasted_iota(jnp.int32, (8, LANES), 0)
    latitude = (lax.broadcasted_iota(jnp.int32, (column, block), 0) // LEVELS).astype(jnp.float32)

    def prepare(b, start, slot, shift):
        t = rows[b, pl.ds(start, LANES), :].T
        pert = t[:members]
        var = jnp.sum(pert * pert, axis=0, keepdims=True) * (1.0 / (members - 1))
        err = t[ERR : ERR + 1]
        total = var + err
        scale = 1.0 / ((members - 1) * total)
        shrink = 1.0 / (1.0 + jnp.sqrt(err / total))
        innovation = t[VAL : VAL + 1] - t[MEAN : MEAN + 1]
        zeros = jnp.zeros((LANES - members - 16, LANES), jnp.bfloat16)
        pad = jnp.zeros((16, LANES), jnp.bfloat16)
        hp[:, pl.ds(slot, LANES)] = jnp.concatenate([pert.astype(jnp.bfloat16), pad, zeros], axis=0)
        tail = jnp.where(sub16 == 0, -innovation, 0.0).astype(jnp.bfloat16)
        rhs[:, pl.ds(slot, LANES)] = jnp.concatenate(
            [(shrink * pert).astype(jnp.bfloat16), tail, zeros], axis=0
        )
        ox = t[XPOS : XPOS + 1] + shift
        oy = t[YPOS : YPOS + 1]
        line[:, pl.ds(slot, LANES)] = jnp.where(
            sub8 == 0, ox, jnp.where(sub8 == 1, oy, jnp.where(sub8 == 2, scale, 0.0))
        )

    def window(first, count, body):
        def step(i, carry):
            at = first + i * per_block
            low, high = at < 0, at >= gx_count
            shift = jnp.where(low, extent, jnp.where(high, -extent, 0.0))
            at = at + jnp.where(low, gx_count, jnp.where(high, -gx_count, 0))
            lanes = pl.ds(pl.multiple_of(at * group, LANES), block)
            body(hp[:, lanes], rhs[:, lanes], line[0:1, lanes], line[1:2, lanes], line[2:3, lanes], shift)
            return carry

        lax.fori_loop(0, count, step, 0)

    def increment(cell_rows, pert, weight, right):
        cov = jnp.dot(cell_rows, pert, preferred_element_type=jnp.float32)
        gain = (cov * weight).astype(jnp.bfloat16)
        return lax.dot_general(
            gain, right, (((1,), (1,)), ((), ())), preferred_element_type=jnp.float32
        )

    z[...] = z_in[...]
    for b in range(batches):
        reach = (radius[b] - 2) // CX + 1
        inverse = 1.0 / jnp.full((1, 1), radius[b], jnp.int32).astype(jnp.float32)
        for g in range(obs // LANES):
            prepare(b, g * LANES, g * LANES, 0.0)
        for g in range((per_block - 1) * group // LANES):
            prepare(b, g * LANES, obs + g * LANES, extent)
        cells[...] = z[...].astype(jnp.bfloat16)

        def local(pert, right, ox, oy, scale, shift):
            by_row = taper(jnp.abs(latitude + (gy * CY).astype(jnp.float32) - oy), inverse) * scale
            for x in range(CX):
                here_x = (gx * CX + x).astype(jnp.float32) + shift
                weight = taper(jnp.abs(here_x - ox), inverse) * by_row
                at = slice(x * column, (x + 1) * column)
                z[at, :] = z[at, :] - increment(cells[at, :], pert, weight, right)

        window(gx - reach, (2 * reach + per_block) // per_block, local)

        later = range(b + 1, batches)
        for nb in later:
            obs_cells[nb] = rows[nb].astype(jnp.bfloat16)

        def one_group(q, carry):
            def remote(pert, right, ox, oy, scale, shift):
                for nb in later:
                    at = pl.ds(pl.multiple_of(q * block, block), block)
                    state = rows[nb, at, :]
                    by_x = taper(jnp.abs(state[:, XPOS : XPOS + 1] + shift - ox), inverse)
                    by_y = taper(jnp.abs(state[:, YPOS : YPOS + 1] - oy), inverse)
                    rows[nb, at, :] = state - increment(
                        obs_cells[nb, at, :], pert, by_x * by_y * scale, right
                    )

            window(q * per_block - reach, (2 * reach + 2 * per_block - 1) // per_block, remote)
            return carry

        if b + 1 < batches:
            lax.fori_loop(0, obs // block, one_group, 0)

    for x in range(CX):
        t = z[x * column : (x + 1) * column, :].T
        out_ref[pl.ds(x, members, stride=CX), :] = t[:members] + t[MEAN : MEAN + 1]


def exchange(rows, gx_count, gy_count):
    gx_bits = [1 << i for i in range(gx_count.bit_length() - 1)]
    gy_bits = [1 << i for i in range(gy_count.bit_length() - 1)]
    steps = [("gx", bit) for bit in reversed(gx_bits[1:])]
    steps += [("gy", bit) for bit in reversed(gy_bits)] + [("gx", bit) for bit in gx_bits[:1]]
    masks = [(0, 0)]
    parts = [rows]
    for axis, bit in steps:
        held = parts[0] if len(parts) == 1 else jnp.concatenate(parts, axis=0)
        size = gx_count if axis == "gx" else gy_count
        other = lax.ppermute(held, axis, [(i, i ^ bit) for i in range(size)])
        parts = [held, other]
        move = (bit, 0) if axis == "gx" else (0, bit)
        masks = masks + [(mx ^ move[0], my ^ move[1]) for mx, my in masks]
    return parts, masks


def per_device(gx_count, gy_count, ensemble, obs_values, obs_error, obs_cell, band_offsets):
    members, rows_here, row_len = ensemble.shape
    batches, obs = obs_cell.shape
    total = rows_here * row_len
    group = gy_count * OBS_DEV
    per_block = max(1, BLOCK_OBS // group)
    padded = obs + (per_block - 1) * group
    pos = jnp.stack([lax.axis_index("gx"), lax.axis_index("gy")]).astype(jnp.int32)
    smem = pl.BlockSpec(memory_space=pltpu.SMEM)
    vmem = pl.BlockSpec(memory_space=pltpu.VMEM)
    flat = ensemble.reshape(members * rows_here, row_len)
    z, own = pl.pallas_call(
        functools.partial(pick_kernel, gx_count, gy_count, members, batches),
        out_shape=(
            jax.ShapeDtypeStruct((total, LANES), jnp.float32),
            jax.ShapeDtypeStruct((batches * OBS_DEV, LANES), jnp.float32),
        ),
        in_specs=[smem, smem, smem, smem, vmem],
        out_specs=(vmem, vmem),
        name="pick",
    )(pos, obs_cell, obs_error, obs_values, flat)
    parts, masks = exchange(own, gx_count, gy_count)
    out = pl.pallas_call(
        functools.partial(sweep_kernel, gx_count, gy_count, members, batches, masks),
        out_shape=jax.ShapeDtypeStruct((members * rows_here, row_len), jnp.float32),
        in_specs=[smem, smem] + [vmem] * (len(parts) + 1),
        out_specs=vmem,
        scratch_shapes=[
            pltpu.VMEM((total, LANES), jnp.float32),
            pltpu.VMEM((total, LANES), jnp.bfloat16),
            pltpu.VMEM((batches, obs, LANES), jnp.float32),
            pltpu.VMEM((batches, obs, LANES), jnp.bfloat16),
            pltpu.VMEM((LANES, padded), jnp.bfloat16),
            pltpu.VMEM((LANES, padded), jnp.bfloat16),
            pltpu.VMEM((8, padded), jnp.float32),
        ],
        name="sweep",
    )(pos, band_offsets, *parts, z)
    return out.reshape(ensemble.shape)


def solution(mesh):
    in_specs = (P(None, "gx", "gy"), P(), P(), P(), P())
    out_specs = P(None, "gx", "gy")
    body = functools.partial(per_device, mesh.shape["gx"], mesh.shape["gy"])
    return jax.shard_map(
        body, mesh=mesh, in_specs=in_specs, out_specs=out_specs, check_vma=False
    )
```

```python
import functools

import jax
import jax.numpy as jnp
from jax import lax
from jax.experimental import pallas as pl
from jax.experimental.pallas import tpu as pltpu
from jax.sharding import PartitionSpec as P

LEVELS = 8
CY = 16
CX = 24
COLUMN = CY * LEVELS
OBS_DEV = 32
LANES = 128
MEAN, ERR = 80, 81
USED = 82
SPILL = LANES - USED
BLOCK_OBS = 256
PICK = 32
COLUMNS = 4
PIECES = 4
RADIUS_MAX = 71
STORED_MAX = 16 << 20
VMEM_LIMIT = 24 << 20
PICK_LIMIT = 60 << 20


class Layout:
    def __init__(self, gx_count, gy_count, batches):
        self.gx, self.gy, self.batches = gx_count, gy_count, batches
        self.group = gy_count * OBS_DEV
        self.per_block = max(1, BLOCK_OBS // self.group)
        self.block = self.per_block * self.group
        self.obs = gx_count * self.group
        self.padded = self.obs + (self.per_block - 1) * self.group
        self.pick_rows = self.per_block * PICK
        self.extent = float(gx_count * CX)
        self.blocks = self.obs // self.block
        self.windows = self.window_count((RADIUS_MAX - 2) // CX + 1)
        size = 2 * self.blocks * self.windows * self.block * self.block
        self.stored = size * sum(range(batches)) <= STORED_MAX

    def window_count(self, reach):
        return (2 * reach + 2 * self.per_block - 1) // self.per_block

    def place(self, at):
        low, high = at < 0, at >= self.gx
        shift = jnp.where(low, self.extent, jnp.where(high, -self.extent, 0.0))
        at = at + jnp.where(low, self.gx, jnp.where(high, -self.gx, 0))
        return pl.ds(pl.multiple_of(at * self.group, LANES), self.block), shift


def iota(shape, dim):
    return lax.broadcasted_iota(jnp.int32, shape, dim)


def dot(a, b):
    return jnp.dot(a, b, preferred_element_type=jnp.float32)


def taper(distance, inverse):
    left = jnp.maximum(1.0 - distance * inverse, 0.0)
    return left * left * (3.0 - 2.0 * left)


def inverse_of(radius):
    return 1.0 / jnp.full((1, 1), radius, jnp.int32).astype(jnp.float32)


def reach_of(radius):
    return (radius - 2) // CX + 1


def place_of(cell, start, lay):
    index = iota(cell.shape, 1) + start
    owner = index // OBS_DEV
    ox = owner // lay.gy * CX + cell // COLUMN
    oy = owner % lay.gy * CY + cell % COLUMN // LEVELS
    return ox.astype(jnp.float32), oy.astype(jnp.float32)


def turn_kernel(members, x_ref, z_ref):
    sub = iota((8, COLUMN), 0)
    for x in range(CX):
        block = x_ref[pl.ds(x, members, stride=CX), :]
        mean = jnp.sum(block, axis=0, keepdims=True) * (1.0 / members)
        rest = jnp.zeros((LANES - members - 8, COLUMN), jnp.float32)
        full = jnp.concatenate([block - mean, jnp.where(sub == 0, mean, 0.0), rest], axis=0)
        z_ref[x * COLUMN : (x + 1) * COLUMN, :] = full.T


def pick_kernel(lay, members, cell_in, error_in, value_in, x_in, own_ref, z_ref, x_ref, cell, error, value, rows, sems):
    small = [(cell_in, cell), (error_in, error), (value_in, value)]
    copies = [pltpu.make_async_copy(a, b, sems.at[i]) for i, (a, b) in enumerate(small)]
    part = x_ref.shape[0] // PIECES
    for i in range(PIECES):
        at = pl.ds(i * part, part)
        copies.append(pltpu.make_async_copy(x_in.at[at, :], x_ref.at[at, :], sems.at[len(small) + i]))
    for copy in copies:
        copy.start()
    for copy in copies:
        copy.wait()
    turn_kernel(members, x_ref, z_ref)
    first = (lax.axis_index("gx") * lay.gy + lax.axis_index("gy")) * OBS_DEV
    lane = iota((1, LANES), 1)
    for b in range(lay.batches):
        for r in range(OBS_DEV):
            row = z_ref[pl.ds(cell[b, first + r], 1), :]
            row = row - jnp.where(lane == MEAN, value[b, first + r], 0.0)
            row = jnp.where(lane == ERR, error[b, first + r], row)
            rows[b * OBS_DEV + r : b * OBS_DEV + r + 1, :] = row
    last = rows[2 * OBS_DEV : 3 * OBS_DEV, :]
    wide = iota((OBS_DEV, LANES), 1)
    own_ref[:OBS_DEV, :] = jnp.where(wide < USED, rows[:OBS_DEV, :], pltpu.roll(last, USED, 1))
    own_ref[OBS_DEV:, :] = jnp.where(wide < USED, rows[OBS_DEV : 2 * OBS_DEV, :], pltpu.roll(last, USED - SPILL, 1))


def fill_picks(lay, batch, cell, pick_x, pick_y, slot):
    diagonal = iota((LANES, LANES), 0) == iota((LANES, LANES), 1)
    lane_x = (iota((LANES, 2 * lay.pick_rows), 1) % lay.pick_rows).astype(jnp.float32)
    lane_y = (iota((LANES, 2 * lay.gy * CY), 1) % (lay.gy * CY)).astype(jnp.float32)
    for c in range(lay.obs // LANES):
        at = slice(c * LANES, (c + 1) * LANES)
        ox, oy = place_of(cell[batch : batch + 1, at], c * LANES, lay)
        g = c * LANES // lay.group
        ox = ox + float(g % lay.per_block * PICK - g * CX)
        both = jnp.sum(jnp.where(diagonal, ox * 1024.0 + oy, 0.0), axis=1, keepdims=True)
        down_x = jnp.floor(both * (1.0 / 1024.0))
        down_y = both - down_x * 1024.0
        pick_x[slot, at, :] = jnp.where(lane_x == down_x, 1.0, 0.0).astype(jnp.bfloat16)
        pick_y[slot, at, :] = jnp.where(lane_y == down_y, 1.0, 0.0).astype(jnp.bfloat16)


def fill_tables(lay, batch, cell, inverse, wx_hi, wx_lo, wy_hi, wy_lo):
    pick_sub = iota((PICK, LANES), 0).astype(jnp.float32)
    lat_sub = iota((lay.gy * CY, LANES), 0).astype(jnp.float32)

    def halves(value, high, low, at):
        top = value.astype(jnp.bfloat16)
        high[at] = top
        low[at] = (value - top.astype(jnp.float32)).astype(jnp.bfloat16)

    for c in range(lay.padded // LANES):
        lanes = slice(c * LANES, (c + 1) * LANES)
        start = c * LANES % lay.obs
        ox, oy = place_of(cell[batch : batch + 1, start : start + LANES], start, lay)
        halves(taper(jnp.abs(lat_sub - oy), inverse), wy_hi, wy_lo, (slice(None), lanes))
        for g in range(lay.gx):
            gap = jnp.abs(pick_sub + float(g * CX) - ox)
            gap = jnp.minimum(gap, jnp.abs(lay.extent - gap))
            halves(taper(gap, inverse), wx_hi, wx_lo, (slice(g * PICK, (g + 1) * PICK), lanes))


def tapers(lay, q, lanes, slots, pick_x, pick_y, wx_hi, wx_lo, wy_hi, wy_lo):
    at = slice(q * lay.block, (q + 1) * lay.block)
    near = slice(q * lay.pick_rows, (q + 1) * lay.pick_rows)

    def join(ref):
        return jnp.concatenate([ref[s, at, :] for s in slots], axis=0)

    by_x = dot(join(pick_x), jnp.concatenate([wx_hi[near, lanes], wx_lo[near, lanes]], axis=0))
    by_y = dot(join(pick_y), jnp.concatenate([wy_hi[:, lanes], wy_lo[:, lanes]], axis=0))
    return by_x * by_y


def table_shapes(lay, slots):
    half = jnp.bfloat16
    return [
        pltpu.VMEM((slots, lay.obs, 2 * lay.pick_rows), half),
        pltpu.VMEM((slots, lay.obs, 2 * lay.gy * CY), half),
        pltpu.VMEM((lay.gx * PICK, lay.padded), half),
        pltpu.VMEM((lay.gx * PICK, lay.padded), half),
        pltpu.VMEM((lay.gy * CY, lay.padded), half),
        pltpu.VMEM((lay.gy * CY, lay.padded), half),
    ]


def taper_kernel(lay, batch, later, radius, cell, w_ref, *scratch):
    pick_x, pick_y = scratch[:2]
    fill_picks(lay, later, cell, pick_x, pick_y, 0)
    fill_tables(lay, batch, cell, inverse_of(radius[batch]), *scratch[2:])
    reach = reach_of(radius[batch])

    def windows(i, carry):
        for q in range(lay.blocks):
            lanes = lay.place((q + i) * lay.per_block - reach)[0]
            w_ref[q, i] = tapers(lay, q, lanes, [0], *scratch).astype(jnp.bfloat16)
        return carry

    lax.fori_loop(0, lay.window_count(reach), windows, 0)


def sweep_kernel(lay, members, masks, pairs, radius, cell, error, *refs):
    parts = len(masks)
    n_w = len(pairs)
    gathered, z_in, stored, out_ref = refs[:parts], refs[parts], refs[parts + 1 : parts + 1 + n_w], refs[parts + 1 + n_w]
    z, cells, rows, obs_cells, hp, rhs, line = refs[parts + 2 + n_w :][:7]
    scratch = refs[parts + 2 + n_w :][7:]
    stored = dict(zip(pairs, stored))
    gx, gy = lax.axis_index("gx"), lax.axis_index("gy")
    batches = lay.batches
    packed = 2 * OBS_DEV

    wide = iota((OBS_DEV, LANES), 1)
    for part, owners in zip(gathered, masks):
        for i, (mx, my) in enumerate(owners):
            owner = (gx ^ mx) * lay.gy + (gy ^ my)
            at = pl.ds(pl.multiple_of(owner * OBS_DEV, OBS_DEV), OBS_DEV)
            a = part[i * packed : i * packed + OBS_DEV, :]
            b = part[i * packed + OBS_DEV : (i + 1) * packed, :]
            rows[0, at, :] = a
            rows[1, at, :] = b
            rows[2, at, :] = jnp.where(wide < SPILL, pltpu.roll(a, SPILL, 1), pltpu.roll(b, 2 * SPILL, 1))

    sub8 = iota((8, LANES), 0)
    lane = iota((LANES, LANES), 1)
    latitude = (iota((COLUMN, lay.block), 0) // LEVELS).astype(jnp.float32)

    def prepare(b, start):
        at = slice(start, start + LANES)
        block = rows[b, at, :]
        turned = block.T
        pert = turned[:members]
        err = error[b : b + 1, at]
        var = jnp.sum(pert * pert, axis=0, keepdims=True) * (1.0 / (members - 1))
        scale = 1.0 / ((members - 1) * (var + err))
        zeros = jnp.zeros((LANES - members, LANES), jnp.bfloat16)
        left = jnp.concatenate([pert.astype(jnp.bfloat16), zeros], axis=0)
        spread = jnp.where(lane < members, block, 0.0)
        var = jnp.sum(spread * spread, axis=1, keepdims=True) * (1.0 / (members - 1))
        err = block[:, ERR : ERR + 1]
        shrink = 1.0 / (1.0 + jnp.sqrt(err / (var + err)))
        right = jnp.where(lane == MEAN, block, shrink * spread).astype(jnp.bfloat16)
        ox, oy = place_of(cell[b : b + 1, at], start, lay)
        for slot, shift in ((start, 0.0), (lay.obs + start, lay.extent)):
            if slot < lay.padded:
                hp[:, slot : slot + LANES] = left
                rhs[slot : slot + LANES, :] = right
                line[:, slot : slot + LANES] = jnp.where(sub8 == 0, ox + shift, jnp.where(sub8 == 1, oy, scale))

    z[...] = z_in[...]
    for b in range(batches):
        reach = reach_of(radius[b])
        inverse = inverse_of(radius[b])
        for g in range(lay.obs // LANES):
            prepare(b, g * LANES)
        cells[...] = z[...].astype(jnp.bfloat16)

        def own_window(i, carry):
            lanes, shift = lay.place(gx - reach + i * lay.per_block)
            pert, right = hp[:, lanes], rhs[lanes, :]
            ox, oy, scale = line[0:1, lanes], line[1:2, lanes], line[2:3, lanes]
            by_row = taper(jnp.abs(latitude + (gy * CY).astype(jnp.float32) - oy), inverse) * scale
            for first in range(0, CX, COLUMNS):
                at = slice(first * COLUMN, (first + COLUMNS) * COLUMN)
                cov = dot(cells[at, :], pert)
                gains = []
                for x in range(COLUMNS):
                    here_x = (gx * CX + first + x).astype(jnp.float32) + shift
                    weight = taper(jnp.abs(here_x - ox), inverse) * by_row
                    gains.append((cov[x * COLUMN : (x + 1) * COLUMN] * weight).astype(jnp.bfloat16))
                z[at, :] = z[at, :] - dot(jnp.concatenate(gains, axis=0), right)
            return carry

        later = range(b + 1, batches)
        for nb in later:
            obs_cells[nb] = rows[nb].astype(jnp.bfloat16)
        if later and not lay.stored:
            for nb in later:
                fill_picks(lay, nb, cell, scratch[0], scratch[1], nb)
            fill_tables(lay, b, cell, inverse, *scratch[2:])

        def group_windows(i, carry):
            for q in range(lay.blocks):
                at = slice(q * lay.block, (q + 1) * lay.block)
                lanes = lay.place((q + i) * lay.per_block - reach)[0]
                if lay.stored:
                    weight = jnp.concatenate([stored[b, nb][q, i] for nb in later], axis=0).astype(jnp.float32)
                else:
                    weight = tapers(lay, q, lanes, later, *scratch)
                cov = dot(jnp.concatenate([obs_cells[nb, at, :] for nb in later], axis=0), hp[:, lanes])
                gain = (weight * line[2:3, lanes] * cov).astype(jnp.bfloat16)
                step = dot(gain, rhs[lanes, :])
                for n, nb in enumerate(later):
                    rows[nb, at, :] = rows[nb, at, :] - step[n * lay.block : (n + 1) * lay.block]
            return carry

        lax.fori_loop(0, (2 * reach + lay.per_block) // lay.per_block, own_window, 0)
        if later:
            lax.fori_loop(0, lay.window_count(reach), group_windows, 0)

    for x in range(CX):
        t = z[x * COLUMN : (x + 1) * COLUMN, :].T
        out_ref[pl.ds(x, members, stride=CX), :] = t[:members] + t[MEAN : MEAN + 1]


def exchange(rows, lay, cell, work):
    def send(held, masks, mx, my):
        n = lay.gx * lay.gy
        pairs = [(i, (i // lay.gy ^ mx) * lay.gy + (i % lay.gy ^ my)) for i in range(n)]
        other = lax.ppermute(held, ("gx", "gy"), pairs)
        return other, [(a ^ mx, b ^ my) for a, b in masks]

    gx_bits = [1 << i for i in range(lay.gx.bit_length() - 1)]
    gy_bits = [1 << i for i in range(lay.gy.bit_length() - 1)]
    masks = [(0, 0)]
    done = []
    steps = [(bit, 0) for bit in reversed(gx_bits[1:])] + [(0, bit) for bit in reversed(gy_bits[2:])]
    for step, (mx, my) in enumerate(steps):
        other, moved = send(rows, masks, mx, my)
        if step < len(work) - 1:
            beside = [f(cell) for f in work[step]]
            other, beside = lax.optimization_barrier((other, beside))
            done += beside
        rows, masks = jnp.concatenate([rows, other], axis=0), masks + moved
        rows, cell = lax.optimization_barrier((rows, cell))
    pieces = [(rows, masks)]
    pieces += [send(rows, masks, 0, my) for my in range(1, min(4, lay.gy))]
    arrived, beside = lax.optimization_barrier(([p for p, _ in pieces[1:]], [f(cell) for f in work[-1]]))
    pieces[1:] = [(p, m) for p, (_, m) in zip(arrived, pieces[1:])]
    done += beside
    pieces += [send(held, owners, bit, 0) for bit in gx_bits[:1] for held, owners in pieces]
    return [p for p, _ in pieces], [m for _, m in pieces], done


def per_device(gx_count, gy_count, ensemble, obs_values, obs_error, obs_cell, band_offsets):
    members, rows_here, row_len = ensemble.shape
    batches = obs_cell.shape[0]
    lay = Layout(gx_count, gy_count, batches)
    total = rows_here * row_len
    smem = pl.BlockSpec(memory_space=pltpu.SMEM)
    vmem = pl.BlockSpec(memory_space=pltpu.VMEM)
    hbm = pl.BlockSpec(memory_space=pl.ANY)
    params = pltpu.CompilerParams(vmem_limit_bytes=VMEM_LIMIT if lay.stored else None)
    flat = ensemble.reshape(members * rows_here, row_len)
    f32, bf16 = jnp.float32, jnp.bfloat16

    def cost(us):
        return pl.CostEstimate(flops=int(us * 1.0e9), bytes_accessed=int(us * 1e5), transcendentals=0)

    own = pl.pallas_call(
        functools.partial(pick_kernel, lay, members),
        out_shape=jax.ShapeDtypeStruct((2 * OBS_DEV, LANES), f32),
        in_specs=[hbm, hbm, hbm, hbm],
        out_specs=vmem,
        scratch_shapes=[
            pltpu.VMEM((total, LANES), f32),
            pltpu.VMEM(flat.shape, f32),
            pltpu.SMEM(obs_cell.shape, jnp.int32),
            pltpu.SMEM(obs_cell.shape, f32),
            pltpu.SMEM(obs_cell.shape, f32),
            pltpu.VMEM((batches * OBS_DEV, LANES), f32),
            pltpu.SemaphoreType.DMA((3 + PIECES,)),
        ],
        compiler_params=pltpu.CompilerParams(vmem_limit_bytes=PICK_LIMIT),
        cost_estimate=cost(2.0),
        name="pick",
    )(obs_cell, obs_error, obs_values, flat)

    def turn(unused):
        return pl.pallas_call(
            functools.partial(turn_kernel, members),
            out_shape=jax.ShapeDtypeStruct((total, LANES), f32),
            in_specs=[vmem],
            out_specs=vmem,
            compiler_params=params,
            cost_estimate=cost(0.5),
            name="turn",
        )(flat)

    def taper_of(b, later):
        return lambda cells: pl.pallas_call(
            functools.partial(taper_kernel, lay, b, later),
            out_shape=jax.ShapeDtypeStruct((lay.blocks, lay.windows, lay.block, lay.block), bf16),
            in_specs=[smem, vmem],
            out_specs=vmem,
            scratch_shapes=table_shapes(lay, 1),
            compiler_params=params,
            cost_estimate=cost(2.5),
            name="tapers",
        )(band_offsets, cells)

    pairs = [(b, later) for b in range(batches) for later in range(b + 1, batches)] if lay.stored else []
    work = [[taper_of(*pair)] for pair in pairs] or [[]]
    work[-1] = work[-1] + [turn]
    parts, masks, (*stored, z) = exchange(own, lay, obs_cell, work)
    out = pl.pallas_call(
        functools.partial(sweep_kernel, lay, members, masks, pairs),
        out_shape=jax.ShapeDtypeStruct((members * rows_here, row_len), f32),
        in_specs=[smem] + [vmem] * (3 + len(parts) + len(stored)),
        out_specs=vmem,
        scratch_shapes=[
            pltpu.VMEM((total, LANES), f32),
            pltpu.VMEM((total, LANES), bf16),
            pltpu.VMEM((batches, lay.obs, LANES), f32),
            pltpu.VMEM((batches, lay.obs, LANES), bf16),
            pltpu.VMEM((LANES, lay.padded), bf16),
            pltpu.VMEM((lay.padded, LANES), bf16),
            pltpu.VMEM((8, lay.padded), f32),
        ]
        + ([] if lay.stored else table_shapes(lay, batches)),
        compiler_params=params,
        cost_estimate=cost(15.0),
        name="sweep",
    )(band_offsets, obs_cell, obs_error, *parts, z, *stored)
    return out.reshape(ensemble.shape)


def solution(mesh):
    in_specs = (P(None, "gx", "gy"), P(), P(), P(), P())
    out_specs = P(None, "gx", "gy")
    body = functools.partial(per_device, mesh.shape["gx"], mesh.shape["gy"])
    return jax.shard_map(
        body, mesh=mesh, in_specs=in_specs, out_specs=out_specs, check_vma=False
    )
```

```python
import functools

import jax
import jax.numpy as jnp
from jax import lax
from jax.experimental import pallas as pl
from jax.experimental.pallas import tpu as pltpu
from jax.sharding import PartitionSpec as P

LEVELS = 8
CY = 16
CX = 24
COLUMN = CY * LEVELS
OBS_DEV = 32
LANES = 128
MEAN, ERR = 80, 81
USED = 82
SPILL = LANES - USED
BLOCK_OBS = 256
COLUMNS = 4
RADIUS_MAX = 71
STORED_MAX = 16 << 20
VMEM_LIMIT = 24 << 20
PICK_LIMIT = 60 << 20


class Layout:
    def __init__(self, gx_count, gy_count, batches):
        self.gx, self.gy, self.batches = gx_count, gy_count, batches
        self.group = gy_count * OBS_DEV
        self.per_block = max(1, BLOCK_OBS // self.group)
        self.block = self.per_block * self.group
        self.obs = gx_count * self.group
        self.padded = self.obs + (self.per_block - 1) * self.group
        self.pick_rows = -(-self.per_block * CX // 16) * 16
        self.extent = float(gx_count * CX)
        self.blocks = self.obs // self.block
        self.windows = self.window_count((RADIUS_MAX - 2) // CX + 1)
        size = 4 * self.blocks * self.windows * self.block * self.block
        self.stored = size * sum(range(batches)) <= STORED_MAX

    def window_count(self, reach):
        return (2 * reach + 2 * self.per_block - 1) // self.per_block

    def place(self, at):
        low, high = at < 0, at >= self.gx
        shift = jnp.where(low, self.extent, jnp.where(high, -self.extent, 0.0))
        at = at + jnp.where(low, self.gx, jnp.where(high, -self.gx, 0))
        return pl.ds(pl.multiple_of(at * self.group, LANES), self.block), shift


def iota(shape, dim):
    return lax.broadcasted_iota(jnp.int32, shape, dim)


def dot(a, b):
    return jnp.dot(a, b, preferred_element_type=jnp.float32)


def taper(distance, inverse):
    left = jnp.maximum(1.0 - distance * inverse, 0.0)
    return left * left * (3.0 - 2.0 * left)


def inverse_of(radius):
    return 1.0 / jnp.full((1, 1), radius, jnp.int32).astype(jnp.float32)


def reach_of(radius):
    return (radius - 2) // CX + 1


def place_of(cell, start, lay):
    index = iota(cell.shape, 1) + start
    owner = index // OBS_DEV
    ox = owner // lay.gy * CX + cell // COLUMN
    oy = owner % lay.gy * CY + cell % COLUMN // LEVELS
    return ox.astype(jnp.float32), oy.astype(jnp.float32)


def turn_column(members, block, z_ref, x):
    mean = jnp.sum(block, axis=0, keepdims=True) * (1.0 / members)
    mean_rows = jnp.where(iota((8, COLUMN), 0) == 0, mean, 0.0)
    rest = jnp.zeros((LANES - members - 8, COLUMN), jnp.float32)
    z_ref[x * COLUMN : (x + 1) * COLUMN, :] = jnp.concatenate([block - mean, mean_rows, rest], axis=0).T


def turn_kernel(members, x_ref, z_ref):
    for x in range(CX):
        turn_column(members, x_ref[pl.ds(x, members, stride=CX), :], z_ref, x)


def pick_kernel(lay, members, cell_in, error_in, value_in, x_in, own_ref, z_ref, x_ref, cell, error, value, rows, sems):
    small = [(cell_in, cell), (error_in, error), (value_in, value)]
    copies = [pltpu.make_async_copy(a, b, sems.at[i]) for i, (a, b) in enumerate(small)]
    for i in range(CX // 8):
        copies.append(pltpu.make_async_copy(x_in.at[:, pl.ds(i * 8, 8), :], x_ref.at[i], sems.at[len(small) + i]))
    for copy in reversed(copies):
        copy.start()
    lines = x_ref.reshape(CX * members, COLUMN)
    for i in reversed(range(CX // 8)):
        copies[len(small) + i].wait()
        for x in range(8):
            turn_column(members, lines[pl.ds(i * 8 * members + x, members, stride=8), :], z_ref, i * 8 + x)
    for copy in copies[: len(small)]:
        copy.wait()
    first = (lax.axis_index("gx") * lay.gy + lax.axis_index("gy")) * OBS_DEV
    lane = iota((1, LANES), 1)
    for b in range(lay.batches):
        for r in range(OBS_DEV):
            row = z_ref[pl.ds(cell[b, first + r], 1), :]
            row = row - jnp.where(lane == MEAN, value[b, first + r], 0.0)
            row = jnp.where(lane == ERR, error[b, first + r], row)
            rows[b * OBS_DEV + r : b * OBS_DEV + r + 1, :] = row
    last = rows[2 * OBS_DEV : 3 * OBS_DEV, :]
    wide = iota((OBS_DEV, LANES), 1)
    own_ref[:OBS_DEV, :] = jnp.where(wide < USED, rows[:OBS_DEV, :], pltpu.roll(last, USED, 1))
    own_ref[OBS_DEV:, :] = jnp.where(wide < USED, rows[OBS_DEV : 2 * OBS_DEV, :], pltpu.roll(last, USED - SPILL, 1))


def fill_picks(lay, batch, cell, pick_x, pick_y, slot):
    diagonal = iota((LANES, LANES), 0) == iota((LANES, LANES), 1)
    lane_x = iota((LANES, lay.pick_rows), 1).astype(jnp.float32)
    lane_y = iota((LANES, lay.gy * CY), 1).astype(jnp.float32)
    for c in range(lay.obs // LANES):
        at = slice(c * LANES, (c + 1) * LANES)
        ox, oy = place_of(cell[batch : batch + 1, at], c * LANES, lay)
        ox = ox - float(c * LANES // lay.block * lay.per_block * CX)
        down_x = jnp.sum(jnp.where(diagonal, ox, 0.0), axis=1, keepdims=True)
        down_y = jnp.sum(jnp.where(diagonal, oy, 0.0), axis=1, keepdims=True)
        pick_x[slot, at, :] = jnp.where(lane_x == down_x, 0.25, 0.0).astype(jnp.bfloat16)
        pick_y[slot, at, :] = jnp.where(lane_y == down_y, 0.25, 0.0).astype(jnp.bfloat16)


def fill_tables(lay, batch, cell, inverse, wx, wy):
    far = (RADIUS_MAX - 2) // CX + 1
    inverse = inverse * 2.0
    pick_sub = iota((lay.pick_rows, LANES), 0).astype(jnp.float32) * inverse
    lat_sub = iota((lay.gy * CY, LANES), 0).astype(jnp.float32) * inverse

    def near(place, at):
        left = jnp.maximum(2.0 - jnp.abs(place - at), 0.0)
        return (left * left * (3.0 - left)).astype(jnp.bfloat16)

    for c in range(lay.padded // LANES):
        lanes = slice(c * LANES, (c + 1) * LANES)
        start = c * LANES % lay.obs
        ox, oy = place_of(cell[batch : batch + 1, start : start + LANES], start, lay)
        wy[:, lanes] = near(lat_sub, oy * inverse)
        for q in range(lay.blocks):
            rows = slice(q * lay.pick_rows, (q + 1) * lay.pick_rows)
            ahead = (start // lay.group - q * lay.per_block + far) % lay.gx - far
            if ahead > far + lay.per_block - 1:
                wx[rows, lanes] = jnp.zeros((lay.pick_rows, LANES), jnp.bfloat16)
                continue
            turn = (start // lay.group - q * lay.per_block - ahead) // lay.gx
            shift = float(q * lay.per_block * CX) + turn * lay.extent
            wx[rows, lanes] = near(pick_sub, (ox - shift) * inverse)


def tapers(lay, q, lanes, slots, pick_x, pick_y, wx, wy):
    at = slice(q * lay.block, (q + 1) * lay.block)

    def join(ref):
        return jnp.concatenate([ref[s, at, :] for s in slots], axis=0)

    return dot(join(pick_x), wx[q * lay.pick_rows : (q + 1) * lay.pick_rows, lanes]) * dot(join(pick_y), wy[:, lanes])


def table_shapes(lay, slots):
    half = jnp.bfloat16
    return [
        pltpu.VMEM((slots, lay.obs, lay.pick_rows), half),
        pltpu.VMEM((slots, lay.obs, lay.gy * CY), half),
        pltpu.VMEM((lay.blocks * lay.pick_rows, lay.padded), half),
        pltpu.VMEM((lay.gy * CY, lay.padded), half),
    ]


def taper_kernel(lay, batch, radius, cell, w_ref, *scratch):
    pick_x, pick_y = scratch[:2]
    slots = range(lay.batches - batch - 1)
    for slot in slots:
        fill_picks(lay, batch + 1 + slot, cell, pick_x, pick_y, slot)
    fill_tables(lay, batch, cell, inverse_of(radius[batch]), *scratch[2:])
    reach = reach_of(radius[batch])

    def windows(i, carry):
        for q in range(lay.blocks):
            lanes = lay.place((q + i) * lay.per_block - reach)[0]
            w_ref[q, i] = tapers(lay, q, lanes, slots, *scratch)
        return carry

    lax.fori_loop(0, lay.window_count(reach), windows, 0)


def sweep_kernel(lay, members, masks, n_w, radius, cell, error, *refs):
    parts = len(masks)
    gathered, z_in, stored, out_ref = refs[:parts], refs[parts], refs[parts + 1 : parts + 1 + n_w], refs[parts + 1 + n_w]
    z, cells, rows, obs_cells, hp, rhs, line = refs[parts + 2 + n_w :][:7]
    scratch = refs[parts + 2 + n_w :][7:]
    gx, gy = lax.axis_index("gx"), lax.axis_index("gy")
    batches = lay.batches
    packed = 2 * OBS_DEV

    wide = iota((OBS_DEV, LANES), 1)
    for part, owners in zip(gathered, masks):
        for i, (mx, my) in enumerate(owners):
            owner = (gx ^ mx) * lay.gy + (gy ^ my)
            at = pl.ds(pl.multiple_of(owner * OBS_DEV, OBS_DEV), OBS_DEV)
            a = part[i * packed : i * packed + OBS_DEV, :]
            b = part[i * packed + OBS_DEV : (i + 1) * packed, :]
            rows[0, at, :] = a
            rows[1, at, :] = b
            rows[2, at, :] = jnp.where(wide < SPILL, pltpu.roll(a, SPILL, 1), pltpu.roll(b, 2 * SPILL, 1))

    sub8 = iota((8, LANES), 0)
    lane = iota((LANES, LANES), 1)
    diagonal = iota((LANES, LANES), 0) == lane
    latitude = (iota((COLUMN, lay.block), 0) // LEVELS).astype(jnp.float32)
    inverses = [inverse_of(radius[b]) for b in range(batches)]
    reaches = [reach_of(radius[b]) for b in range(batches)]

    def prepare(b):
        zeros = jnp.zeros((LANES - members, LANES), jnp.bfloat16)
        for start in range(0, lay.obs, LANES):
            at = slice(start, start + LANES)
            block = rows[b, at, :]
            pert = block.T[:members]
            err = error[b : b + 1, at]
            var = jnp.sum(pert * pert, axis=0, keepdims=True) * (1.0 / (members - 1))
            total = var + err
            scale = 1.0 / ((members - 1) * total)
            shrink = 1.0 / (1.0 + jnp.sqrt(err / total))
            left = jnp.concatenate([pert.astype(jnp.bfloat16), zeros], axis=0)
            down = jnp.sum(jnp.where(diagonal, shrink, 0.0), axis=1, keepdims=True)
            right = jnp.where(lane < members, down * block, jnp.where(lane == MEAN, block, 0.0)).astype(jnp.bfloat16)
            ox, oy = place_of(cell[b : b + 1, at], start, lay)
            for slot, shift in ((start, 0.0), (lay.obs + start, lay.extent)):
                if slot < lay.padded:
                    hp[b % 2, :, slot : slot + LANES] = left
                    rhs[b % 2, slot : slot + LANES, :] = right
                    line[b % 2, :, slot : slot + LANES] = jnp.where(
                        sub8 == 0, ox + shift, jnp.where(sub8 == 1, oy, scale)
                    )

    def output(x):
        t = z[x * COLUMN : (x + 1) * COLUMN, :].T
        out_ref[pl.ds(x, members, stride=CX), :] = t[:members] + t[MEAN : MEAN + 1]

    def own_window(b, i, after=None):
        lanes, shift = lay.place(gx - reaches[b] + i * lay.per_block)
        pert, right = hp[b % 2, :, lanes], rhs[b % 2, lanes, :]
        ox, oy, scale = (line[b % 2, n : n + 1, lanes] for n in range(3))
        by_row = taper(jnp.abs(latitude + (gy * CY).astype(jnp.float32) - oy), inverses[b]) * scale
        for first in range(0, CX, COLUMNS):
            at = slice(first * COLUMN, (first + COLUMNS) * COLUMN)
            cov = dot(cells[at, :], pert)
            gains = []
            for x in range(COLUMNS):
                here_x = (gx * CX + first + x).astype(jnp.float32) + shift
                weight = taper(jnp.abs(here_x - ox), inverses[b]) * by_row
                gains.append((cov[x * COLUMN : (x + 1) * COLUMN] * weight).astype(jnp.bfloat16))
            z[at, :] = z[at, :] - dot(jnp.concatenate(gains, axis=0), right)
            if after is not None:
                for x in range(first, first + COLUMNS):
                    after(x)

    def group_window(b, i):
        later = range(b + 1, batches)
        for q in range(lay.blocks):
            at = slice(q * lay.block, (q + 1) * lay.block)
            lanes = lay.place((q + i) * lay.per_block - reaches[b])[0]
            if lay.stored:
                weight = stored[b][q, i]
            else:
                weight = tapers(lay, q, lanes, later, *scratch)
            cov = dot(jnp.concatenate([obs_cells[nb, at, :] for nb in later], axis=0), hp[b % 2, :, lanes])
            gain = (weight * line[b % 2, 2:3, lanes] * cov).astype(jnp.bfloat16)
            step = dot(gain, rhs[b % 2, lanes, :])
            for n, nb in enumerate(later):
                rows[nb, at, :] = rows[nb, at, :] - step[n * lay.block : (n + 1) * lay.block]

    def loop(start, stop, body):
        def step(i, carry):
            body(i)
            return carry

        lax.fori_loop(start, stop, step, 0)

    z[...] = z_in[...]
    prepare(0)
    for b in range(batches):
        own_count = lay.window_count(reaches[b])
        cells[...] = z[...].astype(jnp.bfloat16)
        if b + 1 < batches:
            for nb in range(b + 1, batches):
                obs_cells[nb] = rows[nb].astype(jnp.bfloat16)
                if not lay.stored:
                    fill_picks(lay, nb, cell, scratch[0], scratch[1], nb)
            if not lay.stored:
                fill_tables(lay, b, cell, inverses[b], *scratch[2:])

            def both(i):
                group_window(b, i)
                own_window(b, i)

            loop(0, own_count - 1, both)
            both(own_count - 1)
            prepare(b + 1)
        else:
            loop(0, own_count - 1, functools.partial(own_window, b))
            own_window(b, own_count - 1, output)


def exchange(rows, lay, cell, work):
    def send(held, masks, mx, my):
        n = lay.gx * lay.gy
        pairs = [(i, (i // lay.gy ^ mx) * lay.gy + (i % lay.gy ^ my)) for i in range(n)]
        other = lax.ppermute(held, ("gx", "gy"), pairs)
        return other, [(a ^ mx, b ^ my) for a, b in masks]

    gx_bits = [1 << i for i in reversed(range(lay.gx.bit_length() - 1))]
    gy_bits = [1 << i for i in reversed(range(lay.gy.bit_length() - 1))]
    core, far = gx_bits[-1:], gx_bits[:-1][:2]

    def all_sums(bits):
        return sorted({sum(b for k, b in enumerate(bits) if n >> k & 1) for n in range(1, 1 << len(bits))})

    steps = [[(m, 0) for m in all_sums(far)]]
    steps += [[(m, 0)] for m in gx_bits[:-1][2:]] + [[(0, m)] for m in gy_bits[:-2]]
    steps += [[(0, m) for m in all_sums(gy_bits[-2:])]]
    masks = [(0, 0)]
    done = []
    for step, moves in enumerate(steps):
        sent = [send(rows, masks, mx, my) for mx, my in moves]
        arrived = [held for held, _ in sent]
        if work and step in (0, len(steps) - 1):
            now, work = (work, []) if step else (work[:1], work[1:])
            arrived, beside = lax.optimization_barrier((arrived, [f(cell) for f in now]))
            done += beside
        pieces = [(rows, masks)] + [(held, owners) for held, (_, owners) in zip(arrived, sent)]
        if step < len(steps) - 1:
            rows, masks = jnp.concatenate([p for p, _ in pieces], axis=0), sum([m for _, m in pieces], [])
            rows, cell = lax.optimization_barrier((rows, cell))
    pieces += [send(held, owners, bit, 0) for bit in core for held, owners in pieces]
    return [p for p, _ in pieces], [m for _, m in pieces], done


def per_device(gx_count, gy_count, ensemble, obs_values, obs_error, obs_cell, band_offsets):
    members, rows_here, row_len = ensemble.shape
    batches = obs_cell.shape[0]
    lay = Layout(gx_count, gy_count, batches)
    total = rows_here * row_len
    smem = pl.BlockSpec(memory_space=pltpu.SMEM)
    vmem = pl.BlockSpec(memory_space=pltpu.VMEM)
    hbm = pl.BlockSpec(memory_space=pl.ANY)
    params = pltpu.CompilerParams(vmem_limit_bytes=VMEM_LIMIT if lay.stored else None)
    flat = ensemble.reshape(members * rows_here, row_len)
    f32, bf16 = jnp.float32, jnp.bfloat16

    def cost(us):
        return pl.CostEstimate(flops=int(us * 1.0e9), bytes_accessed=int(us * 1e5), transcendentals=0)

    own = pl.pallas_call(
        functools.partial(pick_kernel, lay, members),
        out_shape=jax.ShapeDtypeStruct((2 * OBS_DEV, LANES), f32),
        in_specs=[hbm, hbm, hbm, hbm],
        out_specs=vmem,
        scratch_shapes=[
            pltpu.VMEM((total, LANES), f32),
            pltpu.VMEM((CX // 8, members, 8, COLUMN), f32),
            pltpu.SMEM(obs_cell.shape, jnp.int32),
            pltpu.SMEM(obs_cell.shape, f32),
            pltpu.SMEM(obs_cell.shape, f32),
            pltpu.VMEM((batches * OBS_DEV, LANES), f32),
            pltpu.SemaphoreType.DMA((3 + CX // 8,)),
        ],
        compiler_params=pltpu.CompilerParams(vmem_limit_bytes=PICK_LIMIT),
        cost_estimate=cost(2.0),
        name="pick",
    )(obs_cell, obs_error, obs_values, ensemble)

    def turn(unused):
        return pl.pallas_call(
            functools.partial(turn_kernel, members),
            out_shape=jax.ShapeDtypeStruct((total, LANES), f32),
            in_specs=[vmem],
            out_specs=vmem,
            compiler_params=params,
            cost_estimate=cost(0.5),
            name="turn",
        )(flat)

    def taper_of(b):
        later = batches - 1 - b
        return lambda cells: pl.pallas_call(
            functools.partial(taper_kernel, lay, b),
            out_shape=jax.ShapeDtypeStruct((lay.blocks, lay.windows, later * lay.block, lay.block), f32),
            in_specs=[smem, vmem],
            out_specs=vmem,
            scratch_shapes=table_shapes(lay, later),
            compiler_params=params,
            cost_estimate=cost(1.5 + later),
            name="tapers",
        )(band_offsets, cells)

    work = [taper_of(b) for b in range(batches - 1) if lay.stored] + [turn]
    parts, masks, (*stored, z) = exchange(own, lay, obs_cell, work)
    out = pl.pallas_call(
        functools.partial(sweep_kernel, lay, members, masks, len(stored)),
        out_shape=jax.ShapeDtypeStruct((members * rows_here, row_len), f32),
        in_specs=[smem] + [vmem] * (3 + len(parts) + len(stored)),
        out_specs=vmem,
        scratch_shapes=[
            pltpu.VMEM((total, LANES), f32),
            pltpu.VMEM((total, LANES), bf16),
            pltpu.VMEM((batches, lay.obs, LANES), f32),
            pltpu.VMEM((batches, lay.obs, LANES), bf16),
            pltpu.VMEM((2, LANES, lay.padded), bf16),
            pltpu.VMEM((2, lay.padded, LANES), bf16),
            pltpu.VMEM((2, 8, lay.padded), f32),
        ]
        + ([] if lay.stored else table_shapes(lay, batches)),
        compiler_params=params,
        cost_estimate=cost(15.0),
        name="sweep",
    )(band_offsets, obs_cell, obs_error, *parts, z, *stored)
    return out.reshape(ensemble.shape)


def solution(mesh):
    in_specs = (P(None, "gx", "gy"), P(), P(), P(), P())
    out_specs = P(None, "gx", "gy")
    body = functools.partial(per_device, mesh.shape["gx"], mesh.shape["gy"])
    return jax.shard_map(
        body, mesh=mesh, in_specs=in_specs, out_specs=out_specs, check_vma=False
    )
```

```python
import functools

import jax
import jax.numpy as jnp
from jax import lax
from jax.experimental import pallas as pl
from jax.experimental.pallas import tpu as pltpu
from jax.sharding import PartitionSpec as P

LEVELS = 8
CY = 16
CX = 24
COLUMN = CY * LEVELS
OBS_DEV = 32
LANES = 128
MEAN, ERR = 80, 81
USED = 82
SPILL = LANES - USED
BLOCK_OBS = 256
COLUMNS = 4
RADIUS_MAX = 71
STORED_MAX = 16 << 20
VMEM_LIMIT = 24 << 20
PICK_LIMIT = 60 << 20


class Layout:
    def __init__(self, gx_count, gy_count, batches):
        self.gx, self.gy, self.batches = gx_count, gy_count, batches
        self.group = gy_count * OBS_DEV
        self.per_block = max(1, BLOCK_OBS // self.group)
        self.block = self.per_block * self.group
        self.obs = gx_count * self.group
        self.padded = self.obs + (self.per_block - 1) * self.group
        self.pick_rows = -(-self.per_block * CX // 16) * 16
        self.extent = float(gx_count * CX)
        self.blocks = self.obs // self.block
        self.split = self.per_block == 2 and self.group == LANES
        self.windows = self.window_count((RADIUS_MAX - 2) // CX + 1)
        size = 4 * self.blocks * self.windows * self.block * self.block
        self.stored = size * sum(range(batches)) <= STORED_MAX

    def window_count(self, reach):
        return (2 * reach + 2 * self.per_block - 1) // self.per_block

    def pair_window(self, q, i, reach):
        return self.place((q + i) * self.per_block - reach + (1 if self.split else 0))[0]

    def pair_edges(self, q, reach):
        return self.place(2 * q - reach, 1)[0], self.place(2 * q + 1 + reach, 1)[0]

    def place(self, at, count=None):
        low, high = at < 0, at >= self.gx
        shift = jnp.where(low, self.extent, jnp.where(high, -self.extent, 0.0))
        at = at + jnp.where(low, self.gx, jnp.where(high, -self.gx, 0))
        return pl.ds(pl.multiple_of(at * self.group, LANES), (count or self.per_block) * self.group), shift


def iota(shape, dim):
    return lax.broadcasted_iota(jnp.int32, shape, dim)


def dot(a, b):
    return jnp.dot(a, b, preferred_element_type=jnp.float32)


def taper(distance, inverse):
    left = jnp.maximum(1.0 - distance * inverse, 0.0)
    return left * left * (3.0 - 2.0 * left)


def diagonal_pair(a, b):
    none = jnp.zeros_like(a)
    return jnp.concatenate([jnp.concatenate([a, none], axis=1), jnp.concatenate([none, b], axis=1)], axis=0)


def inverse_of(radius):
    return 1.0 / jnp.full((1, 1), radius, jnp.int32).astype(jnp.float32)


def reach_of(radius):
    return (radius - 2) // CX + 1


def place_of(cell, start, lay):
    index = iota(cell.shape, 1) + start
    owner = index // OBS_DEV
    ox = owner // lay.gy * CX + cell // COLUMN
    oy = owner % lay.gy * CY + cell % COLUMN // LEVELS
    return ox.astype(jnp.float32), oy.astype(jnp.float32)


def turn_column(members, block, z_ref, x):
    mean = jnp.sum(block, axis=0, keepdims=True) * (1.0 / members)
    mean_rows = jnp.where(iota((8, COLUMN), 0) == 0, mean, 0.0)
    rest = jnp.zeros((LANES - members - 8, COLUMN), jnp.float32)
    z_ref[x * COLUMN : (x + 1) * COLUMN, :] = jnp.concatenate([block - mean, mean_rows, rest], axis=0).T


def turn_kernel(members, x_ref, z_ref):
    for x in range(CX):
        turn_column(members, x_ref[pl.ds(x, members, stride=CX), :], z_ref, x)


def pick_kernel(lay, members, cell_in, error_in, value_in, x_in, own_ref, z_ref, x_ref, cell, error, value, rows, sems):
    small = [(cell_in, cell), (error_in, error), (value_in, value)]
    copies = [pltpu.make_async_copy(a, b, sems.at[i]) for i, (a, b) in enumerate(small)]
    for i in range(CX // 8):
        copies.append(pltpu.make_async_copy(x_in.at[:, pl.ds(i * 8, 8), :], x_ref.at[i], sems.at[len(small) + i]))
    for copy in reversed(copies):
        copy.start()
    lines = x_ref.reshape(CX * members, COLUMN)
    for i in reversed(range(CX // 8)):
        copies[len(small) + i].wait()
        for x in range(8):
            turn_column(members, lines[pl.ds(i * 8 * members + x, members, stride=8), :], z_ref, i * 8 + x)
    for copy in copies[: len(small)]:
        copy.wait()
    first = (lax.axis_index("gx") * lay.gy + lax.axis_index("gy")) * OBS_DEV
    lane = iota((1, LANES), 1)
    for b in range(lay.batches):
        for r in range(OBS_DEV):
            row = z_ref[pl.ds(cell[b, first + r], 1), :]
            row = row - jnp.where(lane == MEAN, value[b, first + r], 0.0)
            row = jnp.where(lane == ERR, error[b, first + r], row)
            rows[b * OBS_DEV + r : b * OBS_DEV + r + 1, :] = row
    last = rows[2 * OBS_DEV : 3 * OBS_DEV, :]
    wide = iota((OBS_DEV, LANES), 1)
    own_ref[:OBS_DEV, :] = jnp.where(wide < USED, rows[:OBS_DEV, :], pltpu.roll(last, USED, 1))
    own_ref[OBS_DEV:, :] = jnp.where(wide < USED, rows[OBS_DEV : 2 * OBS_DEV, :], pltpu.roll(last, USED - SPILL, 1))


def fill_picks(lay, batch, cell, pick_x, pick_y, slot):
    diagonal = iota((LANES, LANES), 0) == iota((LANES, LANES), 1)
    lane_x = iota((LANES, lay.pick_rows), 1).astype(jnp.float32)
    lane_y = iota((LANES, lay.gy * CY), 1).astype(jnp.float32)
    for c in range(lay.obs // LANES):
        at = slice(c * LANES, (c + 1) * LANES)
        ox, oy = place_of(cell[batch : batch + 1, at], c * LANES, lay)
        ox = ox - float(c * LANES // lay.block * lay.per_block * CX)
        down_x = jnp.sum(jnp.where(diagonal, ox, 0.0), axis=1, keepdims=True)
        down_y = jnp.sum(jnp.where(diagonal, oy, 0.0), axis=1, keepdims=True)
        pick_x[slot, at, :] = jnp.where(lane_x == down_x, 0.25, 0.0).astype(jnp.bfloat16)
        pick_y[slot, at, :] = jnp.where(lane_y == down_y, 0.25, 0.0).astype(jnp.bfloat16)


def fill_tables(lay, batch, cell, inverse, wx, wy):
    far = (RADIUS_MAX - 2) // CX + 1
    inverse = inverse * 2.0
    pick_sub = iota((lay.pick_rows, LANES), 0).astype(jnp.float32) * inverse
    lat_sub = iota((lay.gy * CY, LANES), 0).astype(jnp.float32) * inverse

    def near(place, at):
        left = jnp.maximum(2.0 - jnp.abs(place - at), 0.0)
        return (left * left * (3.0 - left)).astype(jnp.bfloat16)

    for c in range(lay.padded // LANES):
        lanes = slice(c * LANES, (c + 1) * LANES)
        start = c * LANES % lay.obs
        ox, oy = place_of(cell[batch : batch + 1, start : start + LANES], start, lay)
        wy[:, lanes] = near(lat_sub, oy * inverse)
        for q in range(lay.blocks):
            rows = slice(q * lay.pick_rows, (q + 1) * lay.pick_rows)
            ahead = (start // lay.group - q * lay.per_block + far) % lay.gx - far
            if ahead > far + lay.per_block - 1:
                wx[rows, lanes] = jnp.zeros((lay.pick_rows, LANES), jnp.bfloat16)
                continue
            turn = (start // lay.group - q * lay.per_block - ahead) // lay.gx
            shift = float(q * lay.per_block * CX) + turn * lay.extent
            wx[rows, lanes] = near(pick_sub, (ox - shift) * inverse)


def tapers(lay, q, lanes, slots, pick_x, pick_y, wx, wy, part=None):
    size = lay.block if part is None else lay.group
    first = q * lay.block + (part or 0) * lay.group
    at = slice(first, first + size)

    def join(ref):
        return jnp.concatenate([ref[s, at, :] for s in slots], axis=0)

    return dot(join(pick_x), wx[q * lay.pick_rows : (q + 1) * lay.pick_rows, lanes]) * dot(join(pick_y), wy[:, lanes])


def table_shapes(lay, slots):
    half = jnp.bfloat16
    return [
        pltpu.VMEM((slots, lay.obs, lay.pick_rows), half),
        pltpu.VMEM((slots, lay.obs, lay.gy * CY), half),
        pltpu.VMEM((lay.blocks * lay.pick_rows, lay.padded), half),
        pltpu.VMEM((lay.gy * CY, lay.padded), half),
    ]


def taper_kernel(lay, batch, radius, cell, w_ref, *scratch):
    pick_x, pick_y = scratch[:2]
    slots = range(lay.batches - batch - 1)
    for slot in slots:
        fill_picks(lay, batch + 1 + slot, cell, pick_x, pick_y, slot)
    fill_tables(lay, batch, cell, inverse_of(radius[batch]), *scratch[2:])
    reach = reach_of(radius[batch])

    def windows(i, carry):
        for q in range(lay.blocks):
            w_ref[q, i] = tapers(lay, q, lay.pair_window(q, i, reach), slots, *scratch)
        return carry

    if lay.split:
        for q in range(lay.blocks):
            edges = [tapers(lay, q, lanes, slots, *scratch, part=n) for n, lanes in enumerate(lay.pair_edges(q, reach))]
            w_ref[q, lay.windows - 1, : len(slots) * lay.group, :] = jnp.concatenate(edges, axis=1)
    lax.fori_loop(0, lay.window_count(reach) - (1 if lay.split else 0), windows, 0)


def sweep_kernel(lay, members, masks, n_w, radius, cell, error, *refs):
    parts = len(masks)
    gathered, z_in, stored, out_ref = refs[:parts], refs[parts], refs[parts + 1 : parts + 1 + n_w], refs[parts + 1 + n_w]
    z, cells, rows, obs_cells, hp, rhs, line = refs[parts + 2 + n_w :][:7]
    scratch = refs[parts + 2 + n_w :][7:]
    gx, gy = lax.axis_index("gx"), lax.axis_index("gy")
    batches = lay.batches
    packed = 2 * OBS_DEV

    wide = iota((OBS_DEV, LANES), 1)
    for part, owners in zip(gathered, masks):
        for i, (mx, my) in enumerate(owners):
            owner = (gx ^ mx) * lay.gy + (gy ^ my)
            at = pl.ds(pl.multiple_of(owner * OBS_DEV, OBS_DEV), OBS_DEV)
            a = part[i * packed : i * packed + OBS_DEV, :]
            b = part[i * packed + OBS_DEV : (i + 1) * packed, :]
            rows[0, at, :] = a
            rows[1, at, :] = b
            rows[2, at, :] = jnp.where(wide < SPILL, pltpu.roll(a, SPILL, 1), pltpu.roll(b, 2 * SPILL, 1))

    sub8 = iota((8, LANES), 0)
    lane = iota((LANES, LANES), 1)
    diagonal = iota((LANES, LANES), 0) == lane
    latitude = (iota((COLUMN, lay.block), 0) // LEVELS).astype(jnp.float32)
    inverses = [inverse_of(radius[b]) for b in range(batches)]
    reaches = [reach_of(radius[b]) for b in range(batches)]

    def prepare(b):
        zeros = jnp.zeros((LANES - members, LANES), jnp.bfloat16)
        for start in range(0, lay.obs, LANES):
            at = slice(start, start + LANES)
            block = rows[b, at, :]
            pert = block.T[:members]
            err = error[b : b + 1, at]
            var = jnp.sum(pert * pert, axis=0, keepdims=True) * (1.0 / (members - 1))
            total = var + err
            scale = 1.0 / ((members - 1) * total)
            shrink = 1.0 / (1.0 + jnp.sqrt(err / total))
            left = jnp.concatenate([pert.astype(jnp.bfloat16), zeros], axis=0)
            down = jnp.sum(jnp.where(diagonal, shrink, 0.0), axis=1, keepdims=True)
            right = jnp.where(lane < members, down * block, jnp.where(lane == MEAN, block, 0.0)).astype(jnp.bfloat16)
            ox, oy = place_of(cell[b : b + 1, at], start, lay)
            for slot, shift in ((start, 0.0), (lay.obs + start, lay.extent)):
                if slot < lay.padded:
                    hp[b % 2, :, slot : slot + LANES] = left
                    rhs[b % 2, slot : slot + LANES, :] = right
                    line[b % 2, :, slot : slot + LANES] = jnp.where(
                        sub8 == 0, ox + shift, jnp.where(sub8 == 1, oy, scale)
                    )

    def output(x):
        t = z[x * COLUMN : (x + 1) * COLUMN, :].T
        out_ref[pl.ds(x, members, stride=CX), :] = t[:members] + t[MEAN : MEAN + 1]

    def own_window(b, i, after=None):
        lanes, shift = lay.place(gx - reaches[b] + i * lay.per_block)
        pert, right = hp[b % 2, :, lanes], rhs[b % 2, lanes, :]
        ox, oy, scale = (line[b % 2, n : n + 1, lanes] for n in range(3))
        by_row = taper(jnp.abs(latitude + (gy * CY).astype(jnp.float32) - oy), inverses[b]) * scale
        for first in range(0, CX, COLUMNS):
            at = slice(first * COLUMN, (first + COLUMNS) * COLUMN)
            cov = dot(cells[at, :], pert)
            gains = []
            for x in range(COLUMNS):
                here_x = (gx * CX + first + x).astype(jnp.float32) + shift
                weight = taper(jnp.abs(here_x - ox), inverses[b]) * by_row
                gains.append((cov[x * COLUMN : (x + 1) * COLUMN] * weight).astype(jnp.bfloat16))
            z[at, :] = z[at, :] - dot(jnp.concatenate(gains, axis=0), right)
            if after is not None:
                for x in range(first, first + COLUMNS):
                    after(x)

    def half_window(b, i):
        lanes, shift = lay.place(gx + i, 1)
        pert, right = (diagonal_pair(v, v) for v in (hp[b % 2, :, lanes], rhs[b % 2, lanes, :]))
        ox, oy, scale = (line[b % 2, n : n + 1, lanes] for n in range(3))
        by_row = taper(jnp.abs(latitude[:, : lay.group] + (gy * CY).astype(jnp.float32) - oy), inverses[b]) * scale
        half = CX // 2

        def weight(x):
            return taper(jnp.abs((gx * CX + x).astype(jnp.float32) + shift - ox), inverses[b]) * by_row

        for first in range(0, half, COLUMNS):
            at = [slice((n + first) * COLUMN, (n + first + COLUMNS) * COLUMN) for n in (0, half)]
            cov = dot(jnp.concatenate([cells[rows_at, :] for rows_at in at], axis=1), pert)
            gains = []
            for x in range(COLUMNS):
                both = jnp.concatenate([weight(first + x), weight(first + x + half)], axis=1)
                gains.append((cov[x * COLUMN : (x + 1) * COLUMN] * both).astype(jnp.bfloat16))
            step = dot(jnp.concatenate(gains, axis=0), right)
            for n, rows_at in enumerate(at):
                z[rows_at, :] = z[rows_at, :] - step[:, n * LANES : (n + 1) * LANES]

    def group_window(b, i):
        later = range(b + 1, batches)
        for q in range(lay.blocks):
            at = slice(q * lay.block, (q + 1) * lay.block)
            lanes = lay.pair_window(q, i, reaches[b])
            if lay.stored:
                weight = stored[b][q, i]
            else:
                weight = tapers(lay, q, lanes, later, *scratch)
            cov = dot(jnp.concatenate([obs_cells[nb, at, :] for nb in later], axis=0), hp[b % 2, :, lanes])
            gain = (weight * line[b % 2, 2:3, lanes] * cov).astype(jnp.bfloat16)
            step = dot(gain, rhs[b % 2, lanes, :])
            for n, nb in enumerate(later):
                rows[nb, at, :] = rows[nb, at, :] - step[n * lay.block : (n + 1) * lay.block]

    def group_edges(b):
        later = range(b + 1, batches)
        for q in range(lay.blocks):
            at = [slice((2 * q + n) * lay.group, (2 * q + n + 1) * lay.group) for n in range(2)]
            edges = lay.pair_edges(q, reaches[b])
            pert = diagonal_pair(*(hp[b % 2, :, lanes] for lanes in edges))
            right = diagonal_pair(*(rhs[b % 2, lanes, :] for lanes in edges))
            scale = jnp.concatenate([line[b % 2, 2:3, lanes] for lanes in edges], axis=1)
            if lay.stored:
                weight = stored[b][q, lay.windows - 1, : len(later) * lay.group, :]
            else:
                weight = jnp.concatenate(
                    [tapers(lay, q, lanes, later, *scratch, part=n) for n, lanes in enumerate(edges)], axis=1
                )
            state = [jnp.concatenate([obs_cells[nb, rows_at, :] for rows_at in at], axis=1) for nb in later]
            cov = dot(jnp.concatenate(state, axis=0), pert)
            step = dot((weight * scale * cov).astype(jnp.bfloat16), right)
            for m, nb in enumerate(later):
                for n, rows_at in enumerate(at):
                    part = step[m * lay.group : (m + 1) * lay.group, n * LANES : (n + 1) * LANES]
                    rows[nb, rows_at, :] = rows[nb, rows_at, :] - part

    def loop(start, stop, body):
        def step(i, carry):
            body(i)
            return carry

        lax.fori_loop(start, stop, step, 0)

    z[...] = z_in[...]
    prepare(0)
    for b in range(batches):
        last = lay.window_count(reaches[b]) - 1
        cells[...] = z[...].astype(jnp.bfloat16)
        if b + 1 < batches:
            for nb in range(b + 1, batches):
                obs_cells[nb] = rows[nb].astype(jnp.bfloat16)
                if not lay.stored:
                    fill_picks(lay, nb, cell, scratch[0], scratch[1], nb)
            if not lay.stored:
                fill_tables(lay, b, cell, inverses[b], *scratch[2:])

            def both(i):
                group_window(b, i)
                own_window(b, i)

            loop(0, last - 1, both)
            group_window(b, last - 1)
            if lay.split:
                group_edges(b)
            else:
                group_window(b, last)
            own_window(b, last - 1)
            if lay.split:
                half_window(b, reaches[b])
            else:
                own_window(b, last)
            prepare(b + 1)
        else:
            loop(0, last - 1, functools.partial(own_window, b))
            if lay.split:
                half_window(b, reaches[b])
            else:
                own_window(b, last)
            own_window(b, last - 1, output)


def exchange(rows, lay, cell, work):
    def send(held, masks, mx, my):
        n = lay.gx * lay.gy
        pairs = [(i, (i // lay.gy ^ mx) * lay.gy + (i % lay.gy ^ my)) for i in range(n)]
        other = lax.ppermute(held, ("gx", "gy"), pairs)
        return other, [(a ^ mx, b ^ my) for a, b in masks]

    gx_bits = [1 << i for i in reversed(range(lay.gx.bit_length() - 1))]
    gy_bits = [1 << i for i in reversed(range(lay.gy.bit_length() - 1))]
    core, far = gx_bits[-1:], gx_bits[:-1][:2]

    def all_sums(bits):
        return sorted({sum(b for k, b in enumerate(bits) if n >> k & 1) for n in range(1, 1 << len(bits))})

    steps = [[(m, 0) for m in all_sums(far)]]
    steps += [[(m, 0)] for m in gx_bits[:-1][2:]] + [[(0, m)] for m in gy_bits[:-2]]
    steps += [[(0, m) for m in all_sums(gy_bits[-2:])]]
    masks = [(0, 0)]
    done = []
    for step, moves in enumerate(steps):
        sent = [send(rows, masks, mx, my) for mx, my in moves]
        arrived = [held for held, _ in sent]
        if work and step in (0, len(steps) - 1):
            now, work = (work, []) if step else (work[:1], work[1:])
            arrived, beside = lax.optimization_barrier((arrived, [f(cell) for f in now]))
            done += beside
        pieces = [(rows, masks)] + [(held, owners) for held, (_, owners) in zip(arrived, sent)]
        if step < len(steps) - 1:
            rows, masks = jnp.concatenate([p for p, _ in pieces], axis=0), sum([m for _, m in pieces], [])
            rows, cell = lax.optimization_barrier((rows, cell))
    pieces += [send(held, owners, bit, 0) for bit in core for held, owners in pieces]
    return [p for p, _ in pieces], [m for _, m in pieces], done


def per_device(gx_count, gy_count, ensemble, obs_values, obs_error, obs_cell, band_offsets):
    members, rows_here, row_len = ensemble.shape
    batches = obs_cell.shape[0]
    lay = Layout(gx_count, gy_count, batches)
    total = rows_here * row_len
    smem = pl.BlockSpec(memory_space=pltpu.SMEM)
    vmem = pl.BlockSpec(memory_space=pltpu.VMEM)
    hbm = pl.BlockSpec(memory_space=pl.ANY)
    params = pltpu.CompilerParams(vmem_limit_bytes=VMEM_LIMIT if lay.stored else None)
    flat = ensemble.reshape(members * rows_here, row_len)
    f32, bf16 = jnp.float32, jnp.bfloat16

    def cost(us):
        return pl.CostEstimate(flops=int(us * 1.0e9), bytes_accessed=int(us * 1e5), transcendentals=0)

    own = pl.pallas_call(
        functools.partial(pick_kernel, lay, members),
        out_shape=jax.ShapeDtypeStruct((2 * OBS_DEV, LANES), f32),
        in_specs=[hbm, hbm, hbm, hbm],
        out_specs=vmem,
        scratch_shapes=[
            pltpu.VMEM((total, LANES), f32),
            pltpu.VMEM((CX // 8, members, 8, COLUMN), f32),
            pltpu.SMEM(obs_cell.shape, jnp.int32),
            pltpu.SMEM(obs_cell.shape, f32),
            pltpu.SMEM(obs_cell.shape, f32),
            pltpu.VMEM((batches * OBS_DEV, LANES), f32),
            pltpu.SemaphoreType.DMA((3 + CX // 8,)),
        ],
        compiler_params=pltpu.CompilerParams(vmem_limit_bytes=PICK_LIMIT),
        cost_estimate=cost(2.0),
        name="pick",
    )(obs_cell, obs_error, obs_values, ensemble)

    def turn(unused):
        return pl.pallas_call(
            functools.partial(turn_kernel, members),
            out_shape=jax.ShapeDtypeStruct((total, LANES), f32),
            in_specs=[vmem],
            out_specs=vmem,
            compiler_params=params,
            cost_estimate=cost(0.5),
            name="turn",
        )(flat)

    def taper_of(b):
        later = batches - 1 - b
        return lambda cells: pl.pallas_call(
            functools.partial(taper_kernel, lay, b),
            out_shape=jax.ShapeDtypeStruct((lay.blocks, lay.windows, later * lay.block, lay.block), f32),
            in_specs=[smem, vmem],
            out_specs=vmem,
            scratch_shapes=table_shapes(lay, later),
            compiler_params=params,
            cost_estimate=cost(1.5 + later),
            name="tapers",
        )(band_offsets, cells)

    work = [taper_of(b) for b in range(batches - 1) if lay.stored] + [turn]
    parts, masks, (*stored, z) = exchange(own, lay, obs_cell, work)
    out = pl.pallas_call(
        functools.partial(sweep_kernel, lay, members, masks, len(stored)),
        out_shape=jax.ShapeDtypeStruct((members * rows_here, row_len), f32),
        in_specs=[smem] + [vmem] * (3 + len(parts) + len(stored)),
        out_specs=vmem,
        scratch_shapes=[
            pltpu.VMEM((total, LANES), f32),
            pltpu.VMEM((total, LANES), bf16),
            pltpu.VMEM((batches, lay.obs, LANES), f32),
            pltpu.VMEM((batches, lay.obs, LANES), bf16),
            pltpu.VMEM((2, LANES, lay.padded), bf16),
            pltpu.VMEM((2, lay.padded, LANES), bf16),
            pltpu.VMEM((2, 8, lay.padded), f32),
        ]
        + ([] if lay.stored else table_shapes(lay, batches)),
        compiler_params=params,
        cost_estimate=cost(15.0),
        name="sweep",
    )(band_offsets, obs_cell, obs_error, *parts, z, *stored)
    return out.reshape(ensemble.shape)


def solution(mesh):
    in_specs = (P(None, "gx", "gy"), P(), P(), P(), P())
    out_specs = P(None, "gx", "gy")
    body = functools.partial(per_device, mesh.shape["gx"], mesh.shape["gy"])
    return jax.shard_map(
        body, mesh=mesh, in_specs=in_specs, out_specs=out_specs, check_vma=False
    )
```
